32 devices in a mesh: dp: 32 (over z, y, x, core).
Axes of the slice: x: 2, y: 2, z: 4, core: 2. Of those that a mesh axis runs over, the one named last changes fastest.
Arguments:
- images_in: bfloat16 [256, 197, 768], P('dp'), may hold values from -6 to 6
- kept_counts: int32 [256], P('dp'), may hold values from 130 to 196
- patch_index: int32 [256, 196], P('dp'), may hold values from 0 to 195, each once within a row
- out_grad: bfloat16 [256, 256, 768], P('dp'), may hold values from -6 to 6
- w_qkv: bfloat16 [768, 2304], P('dp'), may hold values from -0.21875 to 0.21875
- w_out: bfloat16 [768, 768], P('dp'), may hold values from -1.75 to 1.75
- w_up: bfloat16 [768, 3072], P('dp'), may hold values from -0.21875 to 0.21875
- w_down: bfloat16 [3072, 768], P('dp'), may hold values from -0.109375 to 0.109375
- gain_one: bfloat16 [768], P('dp'), may hold values from 0.25 to 1.75
- gain_two: bfloat16 [768], P('dp'), may hold values from 0.25 to 1.75
- prompts: float32 [768, 50], P('dp'), may hold values from -6 to 6
- momentum: float32 [768, 50], P('dp'), may hold values from -6 to 6
- average: float32 [768, 50], P('dp'), may hold values from -6 to 6
Outputs:
- activations: bfloat16 [256, 256, 768], P('dp')
- input_grad: float32 [256, 197, 768], P('dp')
- prompt_grad: float32 [768, 50], P('dp')
- new_momentum: float32 [768, 50], P('dp')
- new_average: float32 [768, 50], P('dp')
- new_prompts: float32 [768, 50], P('dp')
The draws below stay inside these ranges and needn't reach their ends.
Inputs may be any that keep to these rules, and one draw needn't show every extreme that they name: `kept_counts`: the kept count of each image is at least 2 * 196 // 3 (two thirds of 196, rounded down) and at most 196. Each row of patch_index names every patch number once.
All inputs are finite; a program needn't handle non-finite values.
Results may differ from the reference program's by a relative error of at most 0.011.
Values may be sent and summed in bfloat16 or wider, within the bound.
A program may use at most 192 MiB of HBM per device.

```python
import math
import jax
import jax.numpy as jnp
from jax import lax

D = 768
HEADS = 12
HD = 64
FF = 3072
NPR = 50
NP = 196
SEQ = 256
IMAGES = 256
NTOK = 197


def set_ends(array, key, low, largest):
    shape = array.shape
    place = [jax.random.randint(jax.random.fold_in(key, axis), (), 0, shape[axis]) for axis in range(len(shape))]
    array = array.at[tuple(place)].set(low)
    longest = shape.index(max(shape))
    place[longest] = (place[longest] + 1) % shape[longest]
    return array.at[tuple(place)].set(largest)


def shard_levels(rng, dims, shards, least, top_value):
    factor_of, own = 1.0, jax.random.fold_in(rng, 6)
    for axis_at, blocks in shards:
        draws = jnp.exp(jax.random.uniform(jax.random.fold_in(own, axis_at), (blocks,), jnp.float32, least / len(shards), top_value / len(shards)))
        factor_of = factor_of * jnp.repeat(draws, dims[axis_at] // blocks).reshape([-1 if axis == axis_at else 1 for axis in range(len(dims))])
    return factor_of


def gaussian(stream_key, shape, width, bound, shards=(), kind=jnp.bfloat16):
    entries = width * jax.random.normal(stream_key, shape, jnp.float32)
    if shards:
        entries = entries * shard_levels(stream_key, shape, shards, -0.22, 0.18)
    return jnp.clip(entries, -bound, bound).astype(kind)


def setup_inputs(seed: int = 0) -> dict:
    key_of = jax.random.split(jax.random.key(seed), 14)
    images_in = gaussian(key_of[0], (IMAGES, NTOK, D), 1.0, 6.0, ((0, 32),))
    kept_counts = set_ends(jax.random.randint(key_of[1], (IMAGES,), (2 * NP) // 3, NP + 1), jax.random.fold_in(key_of[1], 1), (2 * NP) // 3, NP).astype(jnp.int32)
    patch_index = jax.vmap(lambda own: jax.random.permutation(own, NP))(jax.random.split(key_of[2], IMAGES)).reshape((IMAGES, NP)).astype(jnp.int32)
    out_grad = gaussian(key_of[3], (IMAGES, SEQ, D), 1.0, 6.0, ((0, 32),))
    w_qkv = gaussian(key_of[4], (D, 3 * D), D ** -0.5, 0.21875, ((0, 32),))
    w_out = gaussian(key_of[5], (D, D), (D // 64) ** -0.5, 1.75, ((0, 32),))
    w_up = gaussian(key_of[6], (D, FF), D ** -0.5, 0.21875, ((0, 32),))
    w_down = gaussian(key_of[7], (FF, D), FF ** -0.5, 0.109375, ((0, 32),))
    gain_one = jnp.clip(1.0 + 0.15 * jax.random.normal(key_of[8], (D,), jnp.float32), 0.25, 1.75).astype(jnp.bfloat16)
    gain_two = jnp.clip(1.0 + 0.15 * jax.random.normal(key_of[9], (D,), jnp.float32), 0.25, 1.75).astype(jnp.bfloat16)
    prompts = gaussian(key_of[10], (D, NPR), 1.0, 6.0, ((0, 32),), jnp.float32)
    momentum = gaussian(key_of[11], (D, NPR), (0.15 * IMAGES ** 0.5), 6.0, ((0, 32),), jnp.float32)
    average = gaussian(key_of[12], (D, NPR), 1.0, 6.0, ((0, 32),), jnp.float32)
    return {"images_in": images_in, "kept_counts": kept_counts, "patch_index": patch_index, "out_grad": out_grad, "w_qkv": w_qkv, "w_out": w_out, "w_up": w_up, "w_down": w_down, "gain_one": gain_one, "gain_two": gain_two, "prompts": prompts, "momentum": momentum, "average": average}


@jax.custom_vjp
def low(v):
    return lax.optimization_barrier(v.astype(jnp.bfloat16)).astype(jnp.float32)

@jax.custom_vjp
def low_back(v):
    return v

def low_keep(v):
    return (low(v), None)

def low_pass(kept, grad):
    return (grad,)

def back_keep(v):
    return (v, None)

def back_low(kept, grad):
    return (low(grad),)
low.defvjp(low_keep, low_pass)
low_back.defvjp(back_keep, back_low)
momentum_coef = 0.9
avg_decay = 0.5
norm_eps = 1e-06
big_negative = -1e+30
highest = lax.Precision.HIGHEST

def layer_norm(values, gain):
    center = values - lax.optimization_barrier(jnp.mean(values, axis=-1, keepdims=True))
    spread = lax.optimization_barrier(jnp.mean(center * center, axis=-1, keepdims=True))
    return center * lax.rsqrt(spread + norm_eps) * gain

def image_forward(prompt_rows, image_rows, kept_count, order_ids, frozen):
    w_qkv, w_out, w_up, w_down, gain_one, gain_two = frozen
    slot_ids = jnp.arange(NP, dtype=jnp.int32)
    select = ((order_ids[:, None] == slot_ids[None, :]) & (slot_ids[:, None] < kept_count)).astype(jnp.float32)
    patches = jnp.dot(select, image_rows[1:], precision=highest)
    filler = jnp.zeros((SEQ - 1 - NPR - NP, D), jnp.float32)
    tokens = jnp.concatenate([image_rows[:1], prompt_rows, patches, filler], axis=0)
    valid_rows = jnp.arange(SEQ, dtype=jnp.int32) < 1 + NPR + kept_count
    normed = low(layer_norm(tokens, gain_one))
    project = low_back(low(jnp.dot(normed, w_qkv, precision=highest)))
    queries = project[:, :D].reshape(SEQ, HEADS, HD)
    keys_all = project[:, D:2 * D].reshape(SEQ, HEADS, HD)
    values_all = project[:, 2 * D:].reshape(SEQ, HEADS, HD)
    raw_scores = jnp.einsum('qhd,khd->hqk', queries, keys_all, precision=highest) * HD ** (-0.5)
    scores = jnp.where(valid_rows[None, None, :], low_back(raw_scores), big_negative)
    row_max = lax.optimization_barrier(jnp.max(scores, axis=-1, keepdims=True))
    exponent = jnp.exp(scores - row_max)
    probs = low(exponent / lax.optimization_barrier(jnp.sum(exponent, axis=-1, keepdims=True)))
    mixed_heads = jnp.einsum('hqk,khd->qhd', probs, values_all, precision=highest).reshape(SEQ, D)
    mixed_heads = low_back(low(mixed_heads))
    middle = tokens + low_back(jnp.dot(mixed_heads, w_out, precision=highest))
    normed_two = low(layer_norm(middle, gain_two))
    hidden = low_back(jnp.dot(normed_two, w_up, precision=highest))
    active = low(jax.nn.gelu(hidden, approximate=False))
    result = middle + low_back(jnp.dot(active, w_down, precision=highest))
    return result * valid_rows[:, None].astype(jnp.float32)

def reference(images_in, kept_counts, patch_index, out_grad, w_qkv, w_out, w_up, w_down, gain_one, gain_two, prompts, momentum, average):
    frozen = tuple((matrix.astype(jnp.float32) for matrix in (w_qkv, w_out, w_up, w_down, gain_one, gain_two)))
    per_group = 16

    def regroup(matrix):
        return matrix.reshape((IMAGES // per_group, per_group) + matrix.shape[1:])

    def group_step(total, pieces):
        image_rows, counts_here, orders_here, cotangent = pieces

        def forward(master, inputs):
            prompt_rows = low(master.T)
            return jax.vmap(lambda image_one, kept_one, order_one: image_forward(prompt_rows, image_one, kept_one, order_one, frozen))(inputs, counts_here, orders_here)
        outputs, pullback = jax.vjp(forward, prompts, image_rows.astype(jnp.float32))
        grad_master, grad_inputs = pullback(cotangent.astype(jnp.float32))
        return (total + grad_master, (outputs.astype(jnp.bfloat16), grad_inputs))
    start = jnp.zeros((D, NPR), jnp.float32)
    prompt_grad, (activations, input_grads) = lax.scan(group_step, start, (regroup(images_in), regroup(kept_counts), regroup(patch_index), regroup(out_grad)))
    rate = 0.5 / math.sqrt(IMAGES)
    new_momentum = momentum_coef * momentum + prompt_grad
    new_prompts = prompts - rate * (prompt_grad + momentum_coef * new_momentum)
    new_average = avg_decay * average + (1.0 - avg_decay) * new_prompts
    return (activations.reshape(IMAGES, SEQ, D), input_grads.reshape(IMAGES, NTOK, D), prompt_grad, new_momentum, new_average, new_prompts)
```

```python
import functools
import math

import jax
import jax.numpy as jnp
from jax import lax
from jax.experimental import pallas as pl
from jax.experimental.pallas import tpu as pltpu
from jax.sharding import PartitionSpec as P

HD = 64
SCORE_SCALE = HD ** (-0.5)
LOG2E = math.log2(math.e)
EPS = 1e-6
MOMENTUM = 0.9
DECAY = 0.5
SRC0 = 56
SURE = 128
LANES = 128
F32 = jnp.float32
BF16 = jnp.bfloat16
MESH = pl.DeviceIdType.MESH
VMEM_LIMIT = 60 << 20


def dot(a, b, ca=1, cb=0):
    return lax.dot_general(a, b, (((ca,), (cb,)), ((), ())), preferred_element_type=F32)


def grid_of(mesh):
    devices = list(mesh.devices.flat)
    try:
        places = [tuple(d.coords)[::-1] + (d.core_on_chip,) for d in devices]
    except AttributeError:
        return None
    low = [min(p[k] for p in places) for k in range(4)]
    size = tuple(max(p[k] for p in places) - low[k] + 1 for k in range(4))
    if math.prod(size) != len(devices) or size[1:] != (2, 2, 2):
        return None
    for i, p in enumerate(places):
        at = 0
        for k in range(4):
            at = at * size[k] + p[k] - low[k]
        if at != i:
            return None
    return size


def gather_kernel(size, pieces, *refs):
    count = len({a for a, _ in pieces})
    ins, outs = refs[:count], refs[count : 2 * count]
    local_sem, send_sem, recv_sem = refs[2 * count :]
    nz, ny, nx, nc = size
    total = nz * ny * nx * nc
    me = lax.axis_index("dp")
    c = lax.rem(me, nc)
    x = lax.rem(me // nc, nx)
    y = lax.rem(me // (nc * nx), ny)
    z = me // (nc * nx * ny)
    plane = nc * nx * ny
    over_z = [lax.rem(me + k * plane, total) for k in range(1, nz)]
    over_y = me + nc * nx * (1 - 2 * y)
    over_x = me + nc * (1 - 2 * x)
    over_c = me + 1 - 2 * c

    barrier = pltpu.get_barrier_semaphore()
    peers = over_z + [over_y, over_x, over_c]
    for peer in peers:
        pl.semaphore_signal(barrier, inc=1, device_id=(peer,), device_id_type=MESH)
    pl.semaphore_wait(barrier, len(peers))

    locals_ = []
    for a in range(count):
        copy = pltpu.make_async_copy(ins[a], outs[a].at[z, y, x, c], local_sem.at[a])
        copy.start()
        locals_.append(copy)

    sends = []

    def send(piece, slot, src, dst, peer):
        copy = pltpu.make_async_remote_copy(
            src_ref=src, dst_ref=dst, send_sem=send_sem.at[piece, slot], recv_sem=recv_sem.at[piece, slot],
            device_id=(peer,), device_id_type=MESH,
        )
        copy.start()
        sends.append(copy)
        return copy

    stage = [{} for _ in pieces]
    for i, (a, cols) in enumerate(pieces):
        stage[i][0] = [
            send(i, k, ins[a].at[:, cols], outs[a].at[z, y, x, c, :, cols], over_z[k]) for k in range(nz - 1)
        ]
    for copy in locals_:
        copy.wait()

    def second(i):
        a, cols = pieces[i]
        for copy in stage[i][0]:
            copy.wait_recv()
        view = outs[a].at[:, y, x, c, :, cols]
        stage[i][1] = send(i, nz - 1, view, view, over_x if i % 2 else over_y)

    def third(i):
        a, cols = pieces[i]
        stage[i][1].wait_recv()
        if i % 2:
            view = outs[a].at[:, y, :, c, :, cols]
            stage[i][2] = send(i, nz, view, view, over_y)
        else:
            view = outs[a].at[:, :, x, c, :, cols]
            stage[i][2] = send(i, nz, view, view, over_x)

    def fourth(i):
        a, cols = pieces[i]
        stage[i][2].wait_recv()
        view = outs[a].at[:, :, :, c, :, cols]
        stage[i][3] = send(i, nz + 1, view, view, over_c)

    n = len(pieces)
    for step in range(n + 4):
        if step < n:
            second(step)
        if 0 <= step - 2 < n:
            third(step - 2)
        if 0 <= step - 4 < n:
            fourth(step - 4)
    for i in range(n):
        stage[i][3].wait_recv()
    for copy in sends:
        copy.wait_send()


def gather_all(size, arrays, parts):
    pieces = []
    for a, (array, number) in enumerate(zip(arrays, parts)):
        width = array.shape[1] // number
        pieces += [(a, pl.ds(k * width, width)) for k in range(number)]
    nz = size[0]
    outs = pl.pallas_call(
        functools.partial(gather_kernel, size, pieces),
        out_shape=[jax.ShapeDtypeStruct(size + a.shape, a.dtype) for a in arrays],
        in_specs=[pl.BlockSpec(memory_space=pl.ANY)] * len(arrays),
        out_specs=[pl.BlockSpec(memory_space=pl.ANY)] * len(arrays),
        scratch_shapes=[
            pltpu.SemaphoreType.DMA((len(arrays),)),
            pltpu.SemaphoreType.DMA((len(pieces), nz + 2)),
            pltpu.SemaphoreType.DMA((len(pieces), nz + 2)),
        ],
        compiler_params=pltpu.CompilerParams(collective_id=0, has_side_effects=True),
        name="gather",
    )(*arrays)
    return [o.reshape((-1, o.shape[-1])) for o in outs]


def sum_kernel(total, part_ref, out_ref, inbox, send_sem, recv_sem):
    me = lax.axis_index("dp")
    others = [lax.rem(me + k, total) for k in range(1, total)]
    barrier = pltpu.get_barrier_semaphore()
    for peer in others:
        pl.semaphore_signal(barrier, inc=1, device_id=(peer,), device_id_type=MESH)
    pl.semaphore_wait(barrier, len(others))
    copies = []
    for k, peer in enumerate(others):
        copy = pltpu.make_async_remote_copy(
            src_ref=part_ref.at[peer],
            dst_ref=inbox.at[k],
            send_sem=send_sem.at[k],
            recv_sem=recv_sem.at[k],
            device_id=(peer,),
            device_id_type=MESH,
        )
        copy.start()
        copies.append(copy)
    grad = part_ref[me]
    for k, copy in enumerate(copies):
        copy.wait_recv()
        grad += inbox[k]
    out_ref[...] = grad
    for copy in copies:
        copy.wait_send()


def sum_over_devices(total, part):
    rows = part.shape[0] // total
    shape = (rows, part.shape[1])
    return pl.pallas_call(
        functools.partial(sum_kernel, total),
        out_shape=jax.ShapeDtypeStruct(shape, part.dtype),
        in_specs=[pl.BlockSpec(memory_space=pltpu.VMEM)],
        out_specs=pl.BlockSpec(memory_space=pltpu.VMEM),
        scratch_shapes=[
            pltpu.VMEM((total - 1,) + shape, part.dtype),
            pltpu.SemaphoreType.DMA((total - 1,)),
            pltpu.SemaphoreType.DMA((total - 1,)),
        ],
        compiler_params=pltpu.CompilerParams(collective_id=1, has_side_effects=True),
        name="sum",
    )(part.reshape((total,) + shape))


def gelu_pair(h):
    t = 1.0 / (1.0 + (0.3275911 * math.sqrt(0.5)) * jnp.abs(h))
    e = jnp.exp2((-0.5 * LOG2E) * (h * h))
    poly = t * (0.127414796 + t * (-0.142248368 + t * (0.7107068705 + t * (-0.7265760135 + t * 0.5307027145))))
    half = poly * e
    cdf = jnp.where(h >= 0, 1.0 - half, half)
    return h * cdf, cdf + h * e * (1.0 / math.sqrt(2.0 * math.pi))


def norm(v):
    center = v - jnp.mean(v, axis=-1, keepdims=True)
    rstd = lax.rsqrt(jnp.mean(center * center, axis=-1, keepdims=True) + EPS)
    return center * rstd, rstd


def norm_back(g, xhat, rstd):
    first = jnp.mean(g, axis=-1, keepdims=True)
    second = jnp.mean(g * xhat, axis=-1, keepdims=True)
    return rstd * (g - first - xhat * second)


def block_kernel(
    npr, heads, ff_chunk,
    kept_ref, img_ref, idx_ref, og_ref, wqkv_ref, wout_ref, wup_ref, wdown_ref, small_ref,
    act_ref, ig_ref, pg_ref,
    row_ref, imgf_ref, back_ref, back_sem, x_ref, gains_ref, proj_ref, projT_ref, e_ref, inv_ref, mixT_ref, res_ref, gn_ref, gprojT_ref, pacc_ref,
):
    b = pl.program_id(0)
    count = pl.num_programs(0)
    seq, width = og_ref.shape[1], og_ref.shape[2]
    npatch = idx_ref.shape[2]
    ntok = npatch + 1
    stride = img_ref.shape[1]
    tiles = width // LANES
    ff = wup_ref.shape[1]

    @pl.when(b == 0)
    def _():
        for t in range(tiles):
            column = img_ref[:, :, t * LANES : t * LANES + LANES].astype(F32)
            imgf_ref[t] = column.reshape(ntok * stride, LANES)
        x_ref[...] = jnp.zeros_like(x_ref)
        small = small_ref[...].astype(F32).T
        x_ref[0:npr, :] = small[0:npr].astype(BF16)
        gains_ref[0:1, :] = small[npr : npr + 1]
        gains_ref[1:2, :] = small[npr + 1 : npr + 2]
        pacc_ref[...] = jnp.zeros_like(pacc_ref)
        row_ref[...] = jnp.zeros_like(row_ref)

    nvalid = 1 + npr + kept_ref[b]
    row_ref[0:1, 0:npatch] = idx_ref[0]
    slot = lax.broadcasted_iota(jnp.int32, row_ref.shape, 1)
    patch = pltpu.roll(row_ref[...], 1 + npr, 1) + (SRC0 + 1)
    source = jnp.where(slot < 1 + npr, slot - 1, jnp.where(slot < nvalid, patch, -1))
    source = jnp.where(slot == 0, SRC0, source)[0:1, :]
    select = (lax.broadcasted_iota(jnp.int32, (seq, seq), 0) == source).astype(F32).astype(BF16)
    for t in range(tiles):
        column = imgf_ref[t, pl.ds(b, ntok, stride=stride), :]
        x_ref[SRC0 : SRC0 + ntok, t * LANES : t * LANES + LANES] = column.astype(BF16)
    tokens = dot(select, x_ref[...], 0, 0)
    xhat1, rstd1 = norm(tokens)
    g1, g2 = gains_ref[0:1, :], gains_ref[1:2, :]
    normed = (xhat1 * g1).astype(BF16)
    for c in range(0, 3 * width, width):
        piece = dot(normed, wqkv_ref[:, c : c + width]).astype(BF16)
        proj_ref[:, c : c + width] = piece
        projT_ref[c : c + width, :] = piece.T
    none = jnp.zeros((HD, seq), BF16)
    tail_valid = lax.broadcasted_iota(jnp.int32, (seq - SURE, seq), 0) + SURE < nvalid

    def in_pair(v, h):
        return jnp.concatenate([none, v] if h % 2 else [v, none], axis=0)

    def pair_columns(group, h):
        at = group * width + 2 * HD * (h // 2)
        return proj_ref[:, at : at + 2 * HD]

    def head_rows(ref, group, h):
        at = group * width + HD * h
        return ref[at : at + HD, :]

    for h in range(heads):
        scores = dot(pair_columns(1, h), in_pair(head_rows(projT_ref, 0, h), h))
        head, tail = scores[:SURE], jnp.where(tail_valid, scores[SURE:], -1e30)
        top = jnp.maximum(jnp.max(head, axis=0, keepdims=True), jnp.max(tail, axis=0, keepdims=True))
        head = jnp.exp2((head - top) * (SCORE_SCALE * LOG2E))
        tail = jnp.exp2((tail - top) * (SCORE_SCALE * LOG2E))
        inv = 1.0 / (jnp.sum(head, axis=0, keepdims=True) + jnp.sum(tail, axis=0, keepdims=True))
        e = jnp.concatenate([head.astype(BF16), tail.astype(BF16)], axis=0)
        e_ref[h] = e
        inv_ref[h] = inv
        mixT_ref[HD * h : HD * h + HD, :] = (dot(head_rows(projT_ref, 2, h), e) * inv).astype(BF16)

    middle = tokens + dot(mixT_ref[...], wout_ref[...], 0, 0)
    xhat2, rstd2 = norm(middle)
    normed2 = (xhat2 * g2).astype(BF16)
    row_valid = lax.broadcasted_iota(jnp.int32, (seq, 1), 0) < nvalid
    grad_result = jnp.where(row_valid, og_ref[0], jnp.zeros_like(og_ref[0]))
    res_ref[...] = middle
    gn_ref[...] = jnp.zeros_like(gn_ref)
    for c in range(0, ff, ff_chunk):
        up = wup_ref[:, c : c + ff_chunk]
        down = wdown_ref[c : c + ff_chunk, :]
        active, slope = gelu_pair(dot(normed2, up))
        res_ref[...] += dot(active.astype(BF16), down)
        gn_ref[...] += dot((dot(grad_result, down, 1, 1) * slope).astype(BF16), up, 1, 1)
    act_ref[0] = jnp.where(row_valid, res_ref[...], 0.0).astype(BF16)
    grad_middle = grad_result.astype(F32) + norm_back(gn_ref[...] * g2, xhat2, rstd2)
    grad_mixT = dot(wout_ref[...], grad_middle.astype(BF16), 1, 1)
    for h in range(heads):
        grad = grad_mixT[HD * h : HD * h + HD, :] * inv_ref[h]
        center = jnp.sum(grad * head_rows(mixT_ref, 0, h).astype(F32), axis=0, keepdims=True)
        grad = grad.astype(BF16)
        grad_probs = dot(pair_columns(2, h), in_pair(grad, h))
        e = e_ref[h]
        grad_scores = (e.astype(F32) * (grad_probs - center)).astype(BF16)
        for group, v in enumerate((
            dot(head_rows(projT_ref, 1, h), grad_scores) * SCORE_SCALE,
            dot(head_rows(projT_ref, 0, h), grad_scores, 1, 1) * SCORE_SCALE,
            dot(grad, e, 1, 1),
        )):
            at = group * width + HD * h
            gprojT_ref[at : at + HD, :] = v.astype(BF16)
    grad_normedT = dot(wqkv_ref[...], gprojT_ref[...])
    grad_tokens = grad_middle + norm_back(grad_normedT.T * g1, xhat1, rstd1)
    high = grad_tokens.astype(BF16)
    low = (grad_tokens - high.astype(F32)).astype(BF16)
    back = dot(select, high) + dot(select, low)
    for t in range(tiles):
        column = back[SRC0 : SRC0 + ntok, t * LANES : t * LANES + LANES]
        back_ref[t, pl.ds(b, ntok, stride=stride), :] = column
    pacc_ref[0:SRC0, :] += back[0:SRC0, :]

    @pl.when(b == count - 1)
    def _():
        copies = []
        for t in range(tiles):
            copy = pltpu.make_async_copy(
                back_ref.at[t].reshape(ntok, stride, LANES),
                ig_ref.at[:, :, t * LANES : t * LANES + LANES],
                back_sem.at[t],
            )
            copy.start()
            copies.append(copy)
        pg_ref[...] = pacc_ref[...].T
        for copy in copies:
            copy.wait()


def block(kept, images, patch_index, out_grad, wqkv, wout, wup, wdown, small, npr, ff_chunk=768):
    count, seq, width = out_grad.shape
    npatch = patch_index.shape[1]
    heads = width // HD
    columns = (width // LANES, images.shape[0] * count, LANES)

    def whole(a):
        return pl.BlockSpec(a.shape, lambda i, *_: (0,) * a.ndim, pipeline_mode=pl.Buffered(1))

    return pl.pallas_call(
        functools.partial(block_kernel, npr, heads, ff_chunk),
        out_shape=(
            jax.ShapeDtypeStruct(out_grad.shape, BF16),
            jax.ShapeDtypeStruct(images.shape, F32),
            jax.ShapeDtypeStruct((width, LANES), F32),
        ),
        grid_spec=pltpu.PrefetchScalarGridSpec(
            num_scalar_prefetch=1,
            grid=(count,),
            in_specs=[
                whole(images),
                pl.BlockSpec((1, 1, npatch), lambda i, *_: (i, 0, 0)),
                pl.BlockSpec((1, seq, width), lambda i, *_: (i, 0, 0)),
                whole(wqkv),
                whole(wout),
                whole(wup),
                whole(wdown),
                whole(small),
            ],
            out_specs=[
                pl.BlockSpec((1, seq, width), lambda i, *_: (i, 0, 0)),
                pl.BlockSpec(memory_space=pl.ANY),
                pl.BlockSpec((width, LANES), lambda i, *_: (0, 0), pipeline_mode=pl.Buffered(1)),
            ],
            scratch_shapes=[
                pltpu.VMEM((8, seq), jnp.int32),
                pltpu.VMEM(columns, F32),
                pltpu.VMEM(columns, F32),
                pltpu.SemaphoreType.DMA((columns[0],)),
                pltpu.VMEM((seq, width), BF16),
                pltpu.VMEM((8, width), F32),
                pltpu.VMEM((seq, 3 * width), BF16),
                pltpu.VMEM((3 * width, seq), BF16),
                pltpu.VMEM((heads, seq, seq), BF16),
                pltpu.VMEM((heads, 1, seq), F32),
                pltpu.VMEM((width, seq), BF16),
                pltpu.VMEM((seq, width), F32),
                pltpu.VMEM((seq, width), F32),
                pltpu.VMEM((3 * width, seq), BF16),
                pltpu.VMEM((LANES, width), F32),
            ],
        ),
        compiler_params=pltpu.CompilerParams(vmem_limit_bytes=VMEM_LIMIT),
        name="block",
    )(kept, images, patch_index.reshape(count, 1, npatch), out_grad, wqkv, wout, wup, wdown, small)


def on_device(
    size, images_in, kept_counts, patch_index, out_grad, w_qkv, w_out, w_up, w_down,
    gain_one, gain_two, prompts, momentum, average,
):
    image_count = images_in.shape[0]
    npr = prompts.shape[1]
    total = lax.axis_size("dp")
    small = jnp.concatenate(
        [prompts.astype(BF16), gain_one[:, None], gain_two[:, None], jnp.zeros((prompts.shape[0], LANES - npr - 2), BF16)],
        axis=1,
    )
    shards = (small, w_qkv, w_out, w_up, w_down)
    near = size is not None and all(a.shape[0] % 8 == 0 for a in shards)
    if near:
        small, wqkv, wout, wup, wdown = gather_all(size, shards, (1, 2, 2, 4, 2))
    else:
        small, wqkv, wout, wup, wdown = (lax.all_gather(a, "dp", axis=0, tiled=True) for a in shards)
    images = jnp.transpose(images_in, (1, 0, 2))
    activations, input_grad, part = block(
        kept_counts, images, patch_index, out_grad, wqkv, wout, wup, wdown, small, npr
    )
    input_grad = jnp.transpose(input_grad, (1, 0, 2))
    if near:
        prompt_grad = sum_over_devices(total, part)[:, :npr]
    else:
        prompt_grad = lax.psum_scatter(part[:, :npr], "dp", scatter_dimension=0, tiled=True)
    scale = 0.5 / math.sqrt(image_count * total)
    new_momentum = MOMENTUM * momentum + prompt_grad
    new_prompts = prompts - scale * (prompt_grad + MOMENTUM * new_momentum)
    new_average = DECAY * average + (1.0 - DECAY) * new_prompts
    return activations, input_grad, prompt_grad, new_momentum, new_average, new_prompts


def solution(mesh):
    return jax.shard_map(
        functools.partial(on_device, grid_of(mesh)),
        mesh=mesh,
        in_specs=(P("dp"),) * 13,
        out_specs=(P("dp"),) * 6,
        check_vma=False,
    )
```
